32 devices in a mesh: vit: 2 (over y), seq: 4 (over z), tensor: 4 (over x, core).
Axes of the slice: x: 2, y: 2, z: 4, core: 2. Of those that a mesh axis runs over, the one named last changes fastest.
Arguments:
- merged: bfloat16 [256, 8192], P(('vit', 'seq'), 'tensor'), may hold values from -6 to 6
- positions: int32 [256], P(('vit', 'seq')), may hold values from 0 to 65535, as said below
- picked: int32 [256], P(('vit', 'seq')), may hold values from 0 to 1, as said below
- router_score: float32 [256], P(('vit', 'seq')), may hold values from -8 to 8
- up_weight: bfloat16 [8192, 16384], P('tensor', ('vit', 'seq')), may hold values from -0.0625 to 0.0625
- down_weight: bfloat16 [16384, 8192], P(('vit', 'seq'), 'tensor'), may hold values from -0.046875 to 0.046875
- mixed_grad: bfloat16 [64, 8192], P(('vit', 'seq'), 'tensor'), may hold values from -6 to 6
Outputs:
- mixed: bfloat16 [64, 8192], P(('vit', 'seq'), 'tensor')
- token_grad: bfloat16 [256, 8192], P(('vit', 'seq'), 'tensor')
- up_grad: float32 [8192, 16384], P('tensor', ('vit', 'seq'))
- down_grad: float32 [16384, 8192], P(('vit', 'seq'), 'tensor')
The draws below stay inside these ranges and needn't reach their ends.
Inputs may be any that keep to these rules, and one draw needn't show every extreme that they name: Among the picked tokens of one aligned block of 32 tokens, at most 2 have the same positions // 16384, and in every block some value of positions // 16384 is shared by exactly 2 picked tokens. `picked`: exactly 8 ones in every aligned block of 32 tokens.
All inputs are finite; a program needn't handle non-finite values.
Results may differ from the reference program's by a relative error of at most 0.0056.
Values may be sent and summed in bfloat16 or wider, within the bound.
No kernel may reach another device: no remote copies, remote signals or barrier semaphores. Data moves between devices by JAX's collectives and lax.ppermute only.
A program may use at most 128 MiB of HBM per device.

```python
import jax
import jax.numpy as jnp
from jax import lax

D = 8192
FF = 16384
CAP = 2
SPAN = 16384
VIS_GRP = 32
PICK = 8
GROUPS = 8
VIS = 256
SLOTS = 64
N_VIT = 2
N_SEQ = 4


def route_group(key):
    keys = jax.random.split(key, 6)
    slot_count = N_SEQ * CAP
    order = jax.random.permutation(keys[0], VIS_GRP)
    slot_ids = jnp.arange(slot_count, dtype=jnp.int32)
    slot_owner = slot_ids // CAP
    ranking = jax.random.permutation(keys[1], N_SEQ).astype(jnp.int32)
    forced = jax.random.randint(keys[2], (), 0, N_SEQ)
    noise = jax.random.randint(keys[3], (slot_count,), 0, 8192)
    scores = (noise + ranking[slot_owner] * 4096 + (slot_owner == forced).astype(jnp.int32) * 1048576) * slot_count + slot_ids
    unused, chosen = lax.top_k(scores, PICK)
    chosen_owner = slot_owner[chosen]
    free_owner = jax.random.randint(keys[4], (VIS_GRP,), 0, N_SEQ)
    owner = free_owner.at[order[:PICK]].set(chosen_owner)
    chosen_flag = jnp.zeros((VIS_GRP,), jnp.int32).at[order[:PICK]].set(1)
    offset = jax.random.randint(keys[5], (VIS_GRP,), 0, SPAN)
    return (owner * SPAN + offset, chosen_flag)


def route_all(key):
    base = jax.random.fold_in(key, 11)
    keys = jax.random.split(base, N_VIT * N_SEQ)
    spots, flags = jax.vmap(route_group)(keys)
    return (spots.reshape(-1).astype(jnp.int32), flags.reshape(-1).astype(jnp.int32))


def draw_positions(key, part):
    return route_all(key)[0]


def draw_picked(key, part):
    return route_all(key)[1]


def shard_levels(stream_key, dims, pieces, low, largest):
    gain, own = 1.0, jax.random.fold_in(stream_key, 6)
    for dim, parts in pieces:
        draws = jnp.exp(jax.random.uniform(jax.random.fold_in(own, dim), (parts,), jnp.float32, low / len(pieces), largest / len(pieces)))
        gain = gain * jnp.repeat(draws, dims[dim] // parts).reshape([-1 if axis == dim else 1 for axis in range(len(dims))])
    return gain


def gaussian(own_key, dims, spread, bound, pieces=(), held_as=jnp.bfloat16):
    values = spread * jax.random.normal(own_key, dims, jnp.float32)
    if pieces:
        values = values * shard_levels(own_key, dims, pieces, -0.22, 0.18)
    return jnp.clip(values, -bound, bound).astype(held_as)


def setup_inputs(seed: int = 0) -> dict:
    splits = jax.random.split(jax.random.key(seed), 8)
    return {
        "merged": gaussian(splits[0], (VIS, D), 1.0, 6.0, ((0, 8), (1, 4))),
        "positions": draw_positions(jax.random.fold_in(splits[7], 71), 0),
        "picked": draw_picked(jax.random.fold_in(splits[7], 71), 0),
        "router_score": gaussian(splits[3], (VIS,), 2.0, 8.0, ((0, 8),), jnp.float32),
        "up_weight": gaussian(splits[4], (D, FF), D ** -0.5, 0.0625, ((0, 4), (1, 8))),
        "down_weight": gaussian(splits[5], (FF, D), FF ** -0.5, 0.046875, ((0, 8), (1, 4))),
        "mixed_grad": gaussian(splits[6], (SLOTS, D), 1.0, 6.0, ((0, 8), (1, 4))),
    }


def blockwise(left, right):
    blocks = N_VIT * N_SEQ
    width = FF // blocks
    rows_count = left.shape[0]
    left_blocks = left.reshape(rows_count, blocks, width).transpose(1, 0, 2)
    right_blocks = right.reshape(blocks, width, right.shape[1])

    def step(total, pair):
        term = jnp.dot(pair[0], pair[1], preferred_element_type=jnp.float32).astype(jnp.bfloat16)
        term = lax.optimization_barrier(term)
        return total + term.astype(jnp.float32), None

    start = jnp.zeros((rows_count, right.shape[1]), jnp.float32)
    total, unused = lax.scan(step, start, (left_blocks, right_blocks))
    return total


def reference(merged, positions, picked, router_score, up_weight, down_weight, mixed_grad):
    slot_count = N_SEQ * CAP
    group = (jnp.arange(VIS, dtype=jnp.int32) // VIS_GRP).astype(jnp.int32)
    target = (positions // SPAN).astype(jnp.int32)
    owners = jnp.arange(N_SEQ, dtype=jnp.int32)
    onehot = (target[:, None] == owners[None, :]).astype(jnp.int32) * picked[:, None]
    stacked = onehot.reshape(GROUPS, VIS_GRP, N_SEQ)
    ranks = jnp.sum((jnp.cumsum(stacked, axis=1) - stacked) * stacked, axis=2).reshape(VIS).astype(jnp.int32)
    owner = (group // N_SEQ) * N_SEQ + target
    slot = owner * slot_count + (group % N_SEQ) * CAP + ranks
    slot = jnp.where(picked == 1, slot, SLOTS).astype(jnp.int32)
    gate_tok = jax.nn.sigmoid(router_score).astype(jnp.bfloat16)
    rows = jnp.zeros((SLOTS, D), jnp.bfloat16).at[slot].set(merged, mode="drop")
    gates = jnp.zeros((SLOTS,), jnp.bfloat16).at[slot].set(gate_tok, mode="drop")
    pre = jnp.dot(rows, up_weight, preferred_element_type=jnp.float32)
    act = jax.nn.silu(pre).astype(jnp.bfloat16)
    y_rows = blockwise(act, down_weight)
    gates_wide = gates.astype(jnp.float32)[:, None]
    mixed = (rows.astype(jnp.float32) + gates_wide * y_rows).astype(jnp.bfloat16)
    scaled = (gates_wide * mixed_grad.astype(jnp.float32)).astype(jnp.bfloat16)
    down_grad = jnp.dot(act.T, scaled, preferred_element_type=jnp.float32)
    act_grad = jnp.dot(scaled, down_weight.T, preferred_element_type=jnp.float32)
    sig = jax.nn.sigmoid(pre)
    pre_grad = (act_grad * sig * (1.0 + pre * (1.0 - sig))).astype(jnp.bfloat16)
    up_grad = jnp.dot(rows.T, pre_grad, preferred_element_type=jnp.float32)
    row_grad = blockwise(pre_grad, up_weight.T)
    slot_grad = (mixed_grad.astype(jnp.float32) + row_grad).astype(jnp.bfloat16)
    safe = jnp.minimum(slot, SLOTS - 1).astype(jnp.int32)
    token_grad = jnp.where(picked[:, None] == 1, slot_grad[safe], jnp.zeros((), jnp.bfloat16)).astype(jnp.bfloat16)
    return mixed, token_grad, up_grad, down_grad
```

```python
import functools

import jax
import jax.numpy as jnp
from jax import lax
from jax.experimental import pallas as pl
from jax.experimental.pallas import tpu as pltpu
from jax.sharding import PartitionSpec as P

CAP = 2
SPAN = 16384
LANES = 128
MIB = 1 << 20

F32 = jnp.float32
BF16 = jnp.bfloat16
VMEM = pltpu.MemorySpace.VMEM
IN_VMEM = pl.BlockSpec(memory_space=VMEM)
IN_HBM = pl.BlockSpec(memory_space=pltpu.MemorySpace.HBM)
IN_PLACE = pl.BlockSpec(memory_space=pl.ANY)
AS_IS = (((1,), (0,)), ((), ()))
TURNED = (((1,), (1,)), ((), ()))


def in_hbm(array):
    return pltpu.with_memory_space_constraint(array, pltpu.MemorySpace.HBM)


def params(mib):
    return pltpu.CompilerParams(vmem_limit_bytes=mib * MIB)


def held(shape, dtype):
    return jax.ShapeDtypeStruct(shape, dtype)


def cost(flops, moved):
    return pl.CostEstimate(flops=int(flops), bytes_accessed=int(moved), transcendentals=0)


def swap(value, axis, bit):
    size = lax.axis_size(axis)
    return lax.ppermute(value, axis, [(i, i ^ bit) for i in range(size)])


def other_half(size):
    return pl.multiple_of((1 - lax.rem(lax.axis_index("tensor"), 2)) * size, size)


def own_half(size):
    return pl.multiple_of(lax.rem(lax.axis_index("tensor"), 2) * size, size)


def load_kernel(parts, half, source, out, sems):
    rows = out.shape[0] // parts
    start = other_half(out.shape[0]) if half else 0
    copies = [
        pltpu.make_async_copy(
            source.at[pl.ds(start + i * rows, rows)], out.at[pl.ds(i * rows, rows)], sems.at[i]
        )
        for i in range(parts)
    ]
    for copy in copies:
        copy.start()
    for copy in copies:
        copy.wait()


def load(weights, half=False):
    rows = weights.shape[0] // 2 if half else weights.shape[0]
    return pl.pallas_call(
        functools.partial(load_kernel, 4, half),
        out_shape=pltpu.VMEM((rows, weights.shape[1]), weights.dtype),
        in_specs=[IN_PLACE],
        out_specs=IN_VMEM,
        scratch_shapes=[pltpu.SemaphoreType.DMA((4,))],
        compiler_params=params(2),
        cost_estimate=cost(0, 2 * rows * weights.shape[1]),
        name="load",
    )(in_hbm(weights))


def gather_pieces(piece, up, down):
    seqs, vits = lax.axis_size("seq"), lax.axis_size("vit")
    piece, up = lax.optimization_barrier((piece, up))
    along = [swap(piece, "seq", k) for k in range(1, seqs)]
    first = [swap(piece, "vit", v) for v in range(1, vits)]
    up = load(up)
    along, up, down = lax.optimization_barrier((along, up, down))
    out = [piece] + along
    for v in range(1, vits):
        out += [first[v - 1]] + [swap(p, "vit", v) for p in along]
    down = load(down, half=True)
    return (out, *lax.optimization_barrier((up, down)))


def sum_over_vit(blocks):
    v = lax.axis_index("vit")
    total = lax.dynamic_index_in_dim(blocks, v, 0, False).astype(F32)
    for k in range(1, lax.axis_size("vit")):
        total = total + swap(lax.dynamic_index_in_dim(blocks, v ^ k, 0, False), "vit", k).astype(F32)
    return total.astype(BF16)


def sum_over_seq(blocks):
    s = lax.axis_index("seq")
    mine = lax.dynamic_index_in_dim(blocks, s, 0, False).astype(F32)
    for k in range(1, lax.axis_size("seq")):
        mine = mine + swap(lax.dynamic_index_in_dim(blocks, s ^ k, 0, False), "seq", k).astype(F32)
    return mine


def route_kernel(seqs, *refs):
    sources, (piece, place), copied, sems = refs[:5], refs[5:7], refs[7:12], refs[12]
    copies = [pltpu.make_async_copy(sources[i], copied[i], sems.at[i]) for i in range(5)]
    for copy in copies:
        copy.start()
    for copy in copies[:3]:
        copy.wait()
    pos, picked, score, merged, cotangent = copied
    local, tokens = place.shape
    width = merged.shape[1]
    taken = picked[...] == 1
    target = lax.shift_right_logical(pos[...], SPAN.bit_length() - 1)
    owner = lax.broadcasted_iota(jnp.int32, (seqs, tokens), 0)
    onehot = jnp.where((owner == target) & taken, 1.0, 0.0)
    before = lax.broadcasted_iota(jnp.int32, (tokens, tokens), 0) < lax.broadcasted_iota(
        jnp.int32, (tokens, tokens), 1
    )
    before = jnp.where(before, 1.0, 0.0).astype(BF16)
    earlier = jnp.dot(onehot.astype(BF16), before, preferred_element_type=F32)
    rank = jnp.sum(earlier * onehot, axis=0, keepdims=True)
    slot = target.astype(F32) * CAP + rank
    wanted = lax.broadcasted_iota(jnp.int32, (local, tokens), 0).astype(F32)
    chosen = jnp.where((wanted == slot) & taken, 1.0, 0.0)
    place[...] = chosen.astype(BF16)
    gate = jax.nn.sigmoid(score[...]).astype(BF16).astype(F32)
    gates = jnp.sum(chosen * gate, axis=1, keepdims=True)
    piece[0:local, width : width + LANES] = jnp.broadcast_to(gates, (local, LANES)).astype(BF16)
    for copy in copies[3:]:
        copy.wait()
    rows = jnp.dot(chosen.astype(BF16), merged[...], preferred_element_type=F32)
    piece[0:local, 0:width] = rows.astype(BF16)
    piece[local : 2 * local, 0:width] = cotangent[...]
    piece[local : 2 * local, width : width + LANES] = jnp.zeros((local, LANES), BF16)


def route(positions, picked, score, merged, cotangent):
    local, width = cotangent.shape
    tokens = merged.shape[0]
    arrays = (positions[None], picked[None], score[None], merged, cotangent)
    return pl.pallas_call(
        functools.partial(route_kernel, lax.axis_size("seq")),
        out_shape=[pltpu.VMEM((2 * local, width + LANES), BF16), held((local, tokens), BF16)],
        in_specs=[IN_HBM] * 5,
        out_specs=[IN_VMEM] * 2,
        scratch_shapes=[pltpu.VMEM(a.shape, a.dtype) for a in arrays] + [pltpu.SemaphoreType.DMA((5,))],
        compiler_params=params(4),
        name="route",
    )(*[in_hbm(a) for a in arrays])


def product(left, weights, turned, start, size, out):
    tile = min(512, size)

    def step(j, carry):
        src = pl.ds(pl.multiple_of(start + j * tile, tile), tile)
        part = weights[src, :] if turned else weights[:, src]
        term = lax.dot_general(left, part, TURNED if turned else AS_IS, preferred_element_type=F32)
        out[:, pl.ds(pl.multiple_of(j * tile, tile), tile)] = term.astype(out.dtype)
        return carry

    lax.fori_loop(0, size // tile, step, 0)


def first_kernel(seqs, count, *refs):
    pieces, up = refs[:count], refs[count]
    rows, scaled, mine, sent, kept, together = refs[count + 1 :]
    slots, width = rows.shape
    local = slots // count
    v, s = lax.axis_index("vit"), lax.axis_index("seq")
    me = v * seqs + s
    for k in range(count):
        together[2 * local * k : 2 * local * (k + 1), :] = pieces[k][...]
    total = 2 * slots
    c = lax.broadcasted_iota(jnp.int32, (1, total), 1)
    dev = (c // (2 * local)) ^ me
    j = c % (2 * local)
    slot_row = ((dev // seqs) * seqs + j // CAP) * local + (dev % seqs) * CAP + j % CAP
    slot = jnp.where(j < local, slot_row, slots + dev * local + j - local)
    wanted = lax.broadcasted_iota(jnp.int32, (total, total), 0)
    order = jnp.where(wanted == slot, 1.0, 0.0).astype(BF16)
    data = together[...]
    got = jnp.dot(order, data, preferred_element_type=F32)
    i = lax.broadcasted_iota(jnp.int32, (2 * local, total), 0)
    own = slots + (v * seqs + (i - local) // CAP) * local + s * CAP + i % CAP
    own = jnp.where(i < local, me * local + i, own)
    pick = jnp.where(own == slot, 1.0, 0.0).astype(BF16)
    mine[...] = jnp.dot(pick, data, preferred_element_type=F32).astype(BF16)
    rows[...] = got[:slots, :width].astype(BF16)
    scaled[...] = (got[:slots, width : width + 1] * got[slots:, :width]).astype(BF16)
    half = sent.shape[1]
    product(rows[...], up, False, other_half(half), half, sent)
    product(rows[...], up, False, own_half(half), half, kept)


def first(pieces, up):
    count = len(pieces)
    two, wide = pieces[0].shape
    slots, width = count * two // 2, wide - LANES
    half = up.shape[1] // 2
    return pl.pallas_call(
        functools.partial(first_kernel, lax.axis_size("seq"), count),
        out_shape=[
            held((slots, width), BF16),
            held((slots, width), BF16),
            held((two, wide), BF16),
            held((slots, half), BF16),
            held((slots, half), F32),
        ],
        in_specs=[IN_VMEM] * (count + 1),
        out_specs=[IN_VMEM] * 5,
        scratch_shapes=[pltpu.VMEM((2 * slots, wide), BF16)],
        compiler_params=params(6 + 30 * slots * wide // MIB),
        cost_estimate=cost(2 * slots * up.size, 2 * up.size),
        name="first",
    )(*pieces, up)


def sent_kernel(scaled, down, sent):
    product(scaled[...], down, True, 0, sent.shape[1], sent)


def sent_act_grad(scaled, down):
    slots, half = scaled.shape[0], down.shape[0]
    return pl.pallas_call(
        sent_kernel,
        out_shape=held((slots, half), BF16),
        in_specs=[IN_VMEM] * 2,
        out_specs=IN_VMEM,
        compiler_params=params(6 + 12 * slots * half // MIB),
        cost_estimate=cost(2 * slots * down.size, 2 * down.size),
        name="sent_act_grad",
    )(scaled, down)


def streamed(left, weights, turned, row, column, chunks, sems, store):
    count = chunks.shape[0]
    tile = chunks.shape[1] if turned else chunks.shape[2]
    deep = left.shape[1]

    def copy(i):
        if turned:
            source = weights.at[pl.ds(row + i * tile, tile), pl.ds(column, deep)]
        else:
            source = weights.at[pl.ds(row, deep), pl.ds(column + i * tile, tile)]
        return pltpu.make_async_copy(source, chunks.at[i], sems.at[i])

    for i in range(count):
        copy(i).start()
    value = left[...]
    for i in range(count):
        copy(i).wait()
        store(
            slice(i * tile, (i + 1) * tile),
            lax.dot_general(
                value, chunks[i], TURNED if turned else AS_IS, preferred_element_type=F32
            ),
        )


def part_kernel(kind, more, seqs, local, *refs):
    left, weights = refs[:2]
    before = refs[2] if "before" in more else None
    y_term = refs[3] if "y" in more else None
    out = refs[2 + len(more)]
    rest = refs[3 + len(more) :]
    chunks, sems = rest[:2]
    slots = left.shape[0]
    there = before is not None
    if kind == "kept":
        turned, row, column = True, own_half(out.shape[1]), 0
    else:
        half = left.shape[1]
        begin = other_half(half) if there else own_half(half)
        turned = kind == "row_grad"
        row, column = (0, begin) if turned else (begin, 0)
    target = rest[2] if y_term is not None else out
    first_row = slots if y_term is not None else 0

    def store(where, value):
        if there:
            value = value + before[:, where]
        target[first_row : first_row + slots, where] = value.astype(target.dtype)

    streamed(left, weights, turned, row, column, chunks, sems, store)
    if y_term is not None:
        target[:slots, :] = y_term[...]
        r = lax.broadcasted_iota(jnp.int32, (2 * slots, 1), 0)
        d, j = r // (2 * local), r % (2 * local)
        src = ((d // seqs) * seqs + (j - local) // CAP) * local + (d % seqs) * CAP + j % CAP
        src = jnp.where(j < local, d * local + j, slots + src)
        order = jnp.where(src == lax.broadcasted_iota(jnp.int32, (2 * slots, 2 * slots), 1), 1.0, 0.0)
        out[...] = jnp.dot(order.astype(BF16), target[...], preferred_element_type=F32).astype(BF16)


def part(kind, left, weights, local, before=None, y_term=None):
    slots, deep = left.shape
    across = {"kept": weights.shape[0] // 2, "y": weights.shape[1], "row_grad": weights.shape[0]}[kind]
    tile = min(512, across)
    count = across // tile
    more = {"before": before, "y": y_term}
    more = {k: v for k, v in more.items() if v is not None}
    joined = y_term is not None
    dtype = BF16 if before is not None else F32
    scratch = [
        pltpu.VMEM((count, deep, tile) if kind == "y" else (count, tile, deep), weights.dtype),
        pltpu.SemaphoreType.DMA((count,)),
    ]
    if joined:
        scratch.append(pltpu.VMEM((2 * slots, across), BF16))
    return pl.pallas_call(
        functools.partial(part_kernel, kind, tuple(more), lax.axis_size("seq"), local),
        out_shape=held((2 * slots if joined else slots, across), dtype),
        in_specs=[IN_VMEM, IN_PLACE] + [IN_VMEM] * len(more),
        out_specs=IN_VMEM,
        scratch_shapes=scratch,
        compiler_params=params(8 + (2 * deep * across + 24 * slots * across) // MIB),
        cost_estimate=cost(2 * slots * deep * across, 2 * deep * across),
        name=kind + ("_other" if before is not None else ""),
    )(left, in_hbm(weights), *more.values())


def down_grad_kernel(own, other, scaled, out, buf, sems):
    half, tile = own.shape[1], buf.shape[1]
    flights = buf.shape[0]
    each = half // tile
    right = scaled[...]

    def copy(i):
        start = (own_half if i < each else other_half)(half) + (i % each) * tile
        return pltpu.make_async_copy(buf.at[i % flights], out.at[pl.ds(start, tile)], sems.at[i % flights])

    outer_steps(2 * each, flights, copy, buf, lambda i: (own if i < each else other)[:, pl.ds((i % each) * tile, tile)], right)


def up_grad_kernel(rows, own, other, out, buf, sems, whole):
    half, tile = own.shape[1], buf.shape[1]
    flights = buf.shape[0]
    whole[:, pl.ds(own_half(half), half)] = own[...]
    whole[:, pl.ds(other_half(half), half)] = other[...]

    def copy(i):
        return pltpu.make_async_copy(
            buf.at[i % flights], out.at[pl.ds(i * tile, tile)], sems.at[i % flights]
        )

    steps = out.shape[0] // tile
    outer_steps(steps, flights, copy, buf, lambda i: rows[:, pl.ds(i * tile, tile)], whole[...])


def outer_steps(steps, flights, copy, buf, left, right):
    for i in range(steps):
        if i >= flights:
            copy(i - flights).wait()
        buf[i % flights] = lax.dot_general(
            left(i), right, (((0,), (0,)), ((), ())), preferred_element_type=F32
        )
        copy(i).start()
    for i in range(max(0, steps - flights), steps):
        copy(i).wait()


def outer(kernel, name, operands, rows, columns, extra=()):
    tile, flights = min(256, rows // 2), 4
    slots = operands[0].shape[0]
    return pl.pallas_call(
        kernel,
        out_shape=held((rows, columns), F32),
        in_specs=[IN_VMEM] * len(operands),
        out_specs=IN_PLACE,
        scratch_shapes=[
            pltpu.VMEM((flights, tile, columns), F32),
            pltpu.SemaphoreType.DMA((flights,)),
            *extra,
        ],
        compiler_params=params(24),
        cost_estimate=cost(2 * slots * rows * columns, 4 * rows * columns),
        name=name,
    )(*operands)


def over_chips(total, bit=2):
    while bit < lax.axis_size("tensor"):
        total = total + swap(total.astype(BF16), "tensor", bit).astype(F32)
        bit *= 2
    return total


def per_device(merged, positions, picked, router_score, up_weight, down_weight, mixed_grad):
    local, width = mixed_grad.shape
    seqs, vits = lax.axis_size("seq"), lax.axis_size("vit")
    hidden = up_weight.shape[1]
    piece, place = route(positions, picked, router_score, merged, mixed_grad)
    pieces, up, down = gather_pieces(piece, up_weight, down_weight)
    rows, scaled, mine, pre_sent, pre_kept = first(pieces, up)
    grad_sent = sent_act_grad(scaled, down)
    grad_got = swap(grad_sent, "tensor", 1)
    pre_sum = pre_kept + swap(pre_sent, "tensor", 1).astype(F32)
    rounded, scaled = lax.optimization_barrier((pre_sum.astype(BF16), scaled))
    grad_kept = part("kept", scaled, down_weight, local)
    pre = over_chips(pre_sum + swap(rounded, "tensor", 2).astype(F32), 4)
    act = jax.nn.silu(pre).astype(BF16)
    act, pre = lax.optimization_barrier((act, pre))
    act_other = swap(act, "tensor", 1)
    y_own = part("y", act, down_weight, local)
    act_grad = over_chips(grad_kept + grad_got.astype(F32))
    act_grad, y_own = lax.optimization_barrier((act_grad, y_own))
    sig = jax.nn.sigmoid(pre)
    pre_grad = (act_grad * sig * (1.0 + pre * (1.0 - sig))).astype(BF16)
    pre_grad_other = swap(pre_grad, "tensor", 1)
    y_term = part("y", act_other, down_weight, local, y_own)
    row_own = part("row_grad", pre_grad, up_weight, local)
    terms = part("row_grad", pre_grad_other, up_weight, local, row_own, y_term)
    down_grad = outer(down_grad_kernel, "down_grad", (act, act_other, scaled), hidden, width)
    terms = sum_over_vit(terms.reshape(vits, seqs, 2 * local, width))
    terms, rows, pre_grad, down_grad = lax.optimization_barrier((terms, rows, pre_grad, down_grad))
    sums = sum_over_seq(terms)
    up_grad = outer(
        up_grad_kernel,
        "up_grad",
        (rows, pre_grad, pre_grad_other),
        width,
        hidden,
        (pltpu.VMEM((rows.shape[0], hidden), BF16),),
    )

    gates = mine[:local, width : width + 1].astype(F32)
    mixed = mine[:local, :width].astype(F32) + gates * sums[:local]
    slot_grad = (mine[local:, :width].astype(F32) + sums[local:]).astype(BF16)
    token_grad = lax.dot_general(
        place, slot_grad, (((0,), (0,)), ((), ())), preferred_element_type=F32
    )
    return (mixed.astype(BF16), token_grad.astype(BF16), up_grad, down_grad)


def solution(mesh):
    return jax.shard_map(
        per_device,
        mesh=mesh,
        in_specs=(
            P(("vit", "seq"), "tensor"),
            P(("vit", "seq")),
            P(("vit", "seq")),
            P(("vit", "seq")),
            P("tensor", ("vit", "seq")),
            P(("vit", "seq"), "tensor"),
            P(("vit", "seq"), "tensor"),
        ),
        out_specs=(
            P(("vit", "seq"), "tensor"),
            P(("vit", "seq"), "tensor"),
            P("tensor", ("vit", "seq")),
            P(("vit", "seq"), "tensor"),
        ),
        check_vma=False,
    )
```

```python
import functools

import jax
import jax.numpy as jnp
from jax import lax
from jax.experimental import pallas as pl
from jax.experimental.pallas import tpu as pltpu
from jax.sharding import PartitionSpec as P


CAP = 2
SPAN = 16384
LANES = 128
MIB = 1 << 20
PARTS = 4

F32 = jnp.float32
BF16 = jnp.bfloat16
VMEM = pltpu.MemorySpace.VMEM
IN_VMEM = pl.BlockSpec(memory_space=VMEM)
IN_HBM = pl.BlockSpec(memory_space=pltpu.MemorySpace.HBM)
IN_PLACE = pl.BlockSpec(memory_space=pl.ANY)
AS_IS = (((1,), (0,)), ((), ()))
TURNED = (((1,), (1,)), ((), ()))


def in_hbm(array):
    return pltpu.with_memory_space_constraint(array, pltpu.MemorySpace.HBM)


def params(mib):
    return pltpu.CompilerParams(vmem_limit_bytes=mib * MIB)


def held(shape, dtype):
    return jax.ShapeDtypeStruct(shape, dtype)


def cost(flops, moved):
    return pl.CostEstimate(flops=int(flops), bytes_accessed=int(moved), transcendentals=0)


def swap(value, axis, bit):
    size = lax.axis_size(axis)
    return lax.ppermute(value, axis, [(i, i ^ bit) for i in range(size)])


def other_half(size):
    return pl.multiple_of((1 - lax.rem(lax.axis_index("tensor"), 2)) * size, size)


def own_half(size):
    return pl.multiple_of(lax.rem(lax.axis_index("tensor"), 2) * size, size)


def load_kernel(wheres, *refs):
    source, outs, sems = refs[0], refs[1:-1], refs[-1]
    copies = []
    for where, out in zip(wheres, outs):
        rows, columns = out.shape
        at = own_half if where == "own" else other_half
        row = at(rows) if rows < source.shape[0] else 0
        column = at(columns) if columns < source.shape[1] else 0
        each = rows // PARTS
        for i in range(PARTS):
            part = source.at[pl.ds(row + i * each, each), pl.ds(column, columns)]
            copies.append(
                pltpu.make_async_copy(part, out.at[pl.ds(i * each, each)], sems.at[len(copies)])
            )
    for copy in copies:
        copy.start()
    for copy in copies:
        copy.wait()


def load(weights, wheres, rows, columns):
    return pl.pallas_call(
        functools.partial(load_kernel, wheres),
        out_shape=[pltpu.VMEM((rows, columns), weights.dtype)] * len(wheres),
        in_specs=[IN_PLACE],
        out_specs=[IN_VMEM] * len(wheres),
        scratch_shapes=[pltpu.SemaphoreType.DMA((PARTS * len(wheres),))],
        compiler_params=params(2),
        cost_estimate=cost(0, 2 * len(wheres) * rows * columns),
        name="load",
    )(in_hbm(weights))


def gather_pieces(piece, up, down):
    seqs, vits = lax.axis_size("seq"), lax.axis_size("vit")
    deep, hidden = up.shape
    piece, up = lax.optimization_barrier((piece, up))
    along = [piece] + [swap(piece, "seq", k) for k in range(1, seqs)]
    near = along[: seqs // 2]
    near, up, down = lax.optimization_barrier((near, up, down))
    (up,) = load(up, ("other",), deep, hidden // 2)
    (sent,) = load(down, ("other",), hidden // 2, deep)
    far, up, sent, down = lax.optimization_barrier((along[seqs // 2 :], up, sent, down))
    along = near + far
    out = list(along)
    for v in range(1, vits):
        out += [swap(p, "vit", v) for p in along]
    (kept,) = load(down, ("own",), hidden // 2, deep)
    return (out, *lax.optimization_barrier((up, sent, kept)))


def sum_over_vit(blocks):
    v = lax.axis_index("vit")
    total = lax.dynamic_index_in_dim(blocks, v, 0, False).astype(F32)
    for k in range(1, lax.axis_size("vit")):
        total = total + swap(lax.dynamic_index_in_dim(blocks, v ^ k, 0, False), "vit", k).astype(F32)
    return total.astype(BF16)


def pieces_over_seq(blocks):
    s = lax.axis_index("seq")
    out = [lax.dynamic_index_in_dim(blocks, s, 0, False)]
    for k in range(1, lax.axis_size("seq")):
        out.append(swap(lax.dynamic_index_in_dim(blocks, s ^ k, 0, False), "seq", k))
    return out


def route_kernel(seqs, *refs):
    sources, (piece, place), copied, sems = refs[:5], refs[5:7], refs[7:12], refs[12]
    copies = [pltpu.make_async_copy(sources[i], copied[i], sems.at[i]) for i in range(5)]
    for copy in copies:
        copy.start()
    for copy in copies[:3]:
        copy.wait()
    pos, picked, score, merged, cotangent = copied
    local, tokens = place.shape
    width = merged.shape[1]
    taken = picked[...] == 1
    target = lax.shift_right_logical(pos[...], SPAN.bit_length() - 1)
    owner = lax.broadcasted_iota(jnp.int32, (seqs, tokens), 0)
    onehot = jnp.where((owner == target) & taken, 1.0, 0.0)
    before = lax.broadcasted_iota(jnp.int32, (tokens, tokens), 0) < lax.broadcasted_iota(
        jnp.int32, (tokens, tokens), 1
    )
    before = jnp.where(before, 1.0, 0.0).astype(BF16)
    earlier = jnp.dot(onehot.astype(BF16), before, preferred_element_type=F32)
    rank = jnp.sum(earlier * onehot, axis=0, keepdims=True)
    slot = target.astype(F32) * CAP + rank
    wanted = lax.broadcasted_iota(jnp.int32, (local, tokens), 0).astype(F32)
    chosen = jnp.where((wanted == slot) & taken, 1.0, 0.0)
    place[...] = chosen.astype(BF16)
    gate = jax.nn.sigmoid(score[...]).astype(BF16).astype(F32)
    gates = jnp.sum(chosen * gate, axis=1, keepdims=True)
    piece[0:local, width : width + LANES] = jnp.broadcast_to(gates, (local, LANES)).astype(BF16)
    for copy in copies[3:]:
        copy.wait()
    rows = jnp.dot(chosen.astype(BF16), merged[...], preferred_element_type=F32)
    piece[0:local, 0:width] = rows.astype(BF16)
    piece[local : 2 * local, 0:width] = cotangent[...]
    piece[local : 2 * local, width : width + LANES] = jnp.zeros((local, LANES), BF16)


def route(positions, picked, score, merged, cotangent):
    local, width = cotangent.shape
    tokens = merged.shape[0]
    arrays = (positions[None], picked[None], score[None], merged, cotangent)
    return pl.pallas_call(
        functools.partial(route_kernel, lax.axis_size("seq")),
        out_shape=[pltpu.VMEM((2 * local, width + LANES), BF16), held((local, tokens), BF16)],
        in_specs=[IN_HBM] * 5,
        out_specs=[IN_VMEM] * 2,
        scratch_shapes=[pltpu.VMEM(a.shape, a.dtype) for a in arrays] + [pltpu.SemaphoreType.DMA((5,))],
        compiler_params=params(4),
        name="route",
    )(*[in_hbm(a) for a in arrays])


def product(left, weights, turned, start, size, out):
    tile = min(512, size)

    def step(j, carry):
        src = pl.ds(pl.multiple_of(start + j * tile, tile), tile)
        part = weights[src, :] if turned else weights[:, src]
        term = lax.dot_general(left, part, TURNED if turned else AS_IS, preferred_element_type=F32)
        out[:, pl.ds(pl.multiple_of(j * tile, tile), tile)] = term.astype(out.dtype)
        return carry

    lax.fori_loop(0, size // tile, step, 0)


def first_kernel(seqs, count, *refs):
    pieces, up_sent, up = refs[:count], refs[count], refs[count + 1]
    rows, scaled, mine, sent, kept, together, chunks, sems = refs[count + 2 :]
    slots, width = rows.shape
    half = sent.shape[1]
    coming = Stream(up, False, 0, own_half(half), chunks, sems)
    local = slots // count
    v, s = lax.axis_index("vit"), lax.axis_index("seq")
    me = v * seqs + s
    for k in range(count):
        together[2 * local * k : 2 * local * (k + 1), :] = pieces[k][...]
    total = 2 * slots
    c = lax.broadcasted_iota(jnp.int32, (1, total), 1)
    dev = (c // (2 * local)) ^ me
    j = c % (2 * local)
    slot_row = ((dev // seqs) * seqs + j // CAP) * local + (dev % seqs) * CAP + j % CAP
    slot = jnp.where(j < local, slot_row, slots + dev * local + j - local)
    wanted = lax.broadcasted_iota(jnp.int32, (total, total), 0)
    order = jnp.where(wanted == slot, 1.0, 0.0).astype(BF16)
    data = together[...]
    got = jnp.dot(order, data, preferred_element_type=F32)
    i = lax.broadcasted_iota(jnp.int32, (2 * local, total), 0)
    own = slots + (v * seqs + (i - local) // CAP) * local + s * CAP + i % CAP
    own = jnp.where(i < local, me * local + i, own)
    pick = jnp.where(own == slot, 1.0, 0.0).astype(BF16)
    mine[...] = jnp.dot(pick, data, preferred_element_type=F32).astype(BF16)
    rows[...] = got[:slots, :width].astype(BF16)
    scaled[...] = (got[:slots, width : width + 1] * got[slots:, :width]).astype(BF16)
    product(rows[...], up_sent, False, 0, half, sent)

    def store(where, value):
        kept[:, where] = value

    coming.finish(rows, store)


def first(pieces, up_sent, up):
    count = len(pieces)
    two, wide = pieces[0].shape
    slots, width = count * two // 2, wide - LANES
    half = up.shape[1] // 2
    return pl.pallas_call(
        functools.partial(first_kernel, lax.axis_size("seq"), count),
        out_shape=[
            held((slots, width), BF16),
            held((slots, width), BF16),
            held((two, wide), BF16),
            held((slots, half), BF16),
            held((slots, half), F32),
        ],
        in_specs=[IN_VMEM] * (count + 1) + [IN_PLACE],
        out_specs=[IN_VMEM] * 5,
        scratch_shapes=[pltpu.VMEM((2 * slots, wide), BF16), *stream_scratch(up, False, width, half)],
        compiler_params=params(6 + (30 * slots * wide + 2 * width * half) // MIB),
        cost_estimate=cost(2 * slots * up.size, 2 * up.size),
        name="first",
    )(*pieces, up_sent, in_hbm(up))


def act_grad_kernel(scaled, down, out, *again):
    if again:
        copy = pltpu.make_async_copy(down, again[0], again[1])
        copy.start()
    product(scaled[...], down, True, 0, out.shape[1], out)
    if again:
        copy.wait()


def act_grad_half(scaled, down, dtype, again=False):
    slots, half = scaled.shape[0], down.shape[0]
    return pl.pallas_call(
        act_grad_kernel,
        out_shape=[held((slots, half), dtype)] + [pltpu.VMEM(down.shape, down.dtype)] * again,
        in_specs=[IN_VMEM] * 2,
        out_specs=[IN_VMEM] * (1 + again),
        scratch_shapes=[pltpu.SemaphoreType.DMA] * again,
        compiler_params=params(6 + 12 * slots * half // MIB),
        cost_estimate=cost(2 * slots * down.size, 2 * down.size),
        name="act_grad",
    )(scaled, down)


class Stream:
    def __init__(self, weights, turned, row, column, chunks, sems):
        self.turned, self.chunks, self.sems = turned, chunks, sems
        count, tall, wide = chunks.shape
        self.copies = []
        for i in range(count):
            begin = (row + i * tall, column) if turned else (row, column + i * wide)
            source = weights.at[pl.ds(begin[0], tall), pl.ds(begin[1], wide)]
            self.copies.append(pltpu.make_async_copy(source, chunks.at[i], sems.at[i]))
        for copy in self.copies:
            copy.start()

    def finish(self, left, store):
        value = left[...]
        _, tall, wide = self.chunks.shape
        tile = tall if self.turned else wide
        for i, copy in enumerate(self.copies):
            copy.wait()
            store(
                slice(i * tile, (i + 1) * tile),
                lax.dot_general(
                    value,
                    self.chunks[i],
                    TURNED if self.turned else AS_IS,
                    preferred_element_type=F32,
                ),
            )


def stream_scratch(weights, turned, deep, across):
    tile = min(512, across)
    count = across // tile
    shape = (count, tile, deep) if turned else (count, deep, tile)
    return [pltpu.VMEM(shape, weights.dtype), pltpu.SemaphoreType.DMA((count,))]


def y_kernel(own, other, down_own, down_other, out):
    y = jnp.dot(own[...], down_own[...], preferred_element_type=F32)
    y = y + jnp.dot(other[...], down_other[...], preferred_element_type=F32)
    out[...] = y.astype(out.dtype)


def y_terms(own, other, down_own, down_other):
    slots, half = own.shape
    width = down_own.shape[1]
    return pl.pallas_call(
        y_kernel,
        out_shape=held((slots, width), BF16),
        in_specs=[IN_VMEM] * 4,
        out_specs=IN_VMEM,
        compiler_params=params(6 + 24 * slots * width // MIB),
        cost_estimate=cost(4 * slots * half * width, 4 * half * width),
        name="y",
    )(own, other, down_own, down_other)


def row_kernel(own, up, out, chunks, sems):
    coming = Stream(up, True, 0, own_half(own.shape[1]), chunks, sems)

    def store(where, value):
        out[:, where] = value

    coming.finish(own, store)


def row_part(own, up):
    slots, half = own.shape
    width = up.shape[0]
    return pl.pallas_call(
        row_kernel,
        out_shape=held((slots, width), F32),
        in_specs=[IN_VMEM, IN_PLACE],
        out_specs=IN_VMEM,
        scratch_shapes=stream_scratch(up, True, half, width),
        compiler_params=params(6 + (up.size + 24 * slots * width) // MIB),
        cost_estimate=cost(slots * up.size, up.size),
        name="row_part",
    )(own, in_hbm(up))


def terms_kernel(seqs, local, other, before, y, up, terms, chunks, sems, term):
    slots, half = other.shape
    coming = Stream(up, True, 0, other_half(half), chunks, sems)
    r = lax.broadcasted_iota(jnp.int32, (2 * slots, 1), 0)
    d, j = r // (2 * local), r % (2 * local)
    src = ((d // seqs) * seqs + (j - local) // CAP) * local + (d % seqs) * CAP + j % CAP
    src = jnp.where(j < local, d * local + j, slots + src)
    order = jnp.where(src == lax.broadcasted_iota(jnp.int32, (2 * slots, 2 * slots), 1), 1.0, 0.0)
    order = order.astype(BF16)
    term[:slots, :] = y[...]

    def store(where, value):
        term[slots:, where] = (value + before[:, where]).astype(BF16)
        both = jnp.dot(order, term[:, where], preferred_element_type=F32)
        terms[:, where] = both.astype(BF16)

    coming.finish(other, store)


def all_terms(other, before, y, up, local):
    slots, half = other.shape
    width = up.shape[0]
    return pl.pallas_call(
        functools.partial(terms_kernel, lax.axis_size("seq"), local),
        out_shape=held((2 * slots, width), BF16),
        in_specs=[IN_VMEM] * 3 + [IN_PLACE],
        out_specs=IN_VMEM,
        scratch_shapes=[
            *stream_scratch(up, True, half, width),
            pltpu.VMEM((2 * slots, width), BF16),
        ],
        compiler_params=params(6 + (up.size + 32 * slots * width) // MIB),
        cost_estimate=cost(slots * up.size, up.size),
        name="all_terms",
    )(other, before, y, in_hbm(up))


def weight_grads_kernel(ahead, begin, *refs):
    if ahead:
        act, act_other, scaled, rows, own, other, down_grad, up_grad, buf, sems, whole = refs
    else:
        rows, own, other, _, up_grad, buf, sems, whole = refs
    half = own.shape[1]
    flights, tile = buf.shape[0], buf.shape[1]
    whole[:, pl.ds(own_half(half), half)] = own[...]
    whole[:, pl.ds(other_half(half), half)] = other[...]
    jobs = []
    if ahead:
        each = half // tile
        for i in range(2 * each):
            left, start = (act, own_half(half)) if i < each else (act_other, other_half(half))
            jobs.append((left, (i % each) * tile, scaled, down_grad, start + (i % each) * tile))
    for i in range(*begin):
        jobs.append((rows, i * tile, whole, up_grad, i * tile))

    def copy(i):
        slot, width = i % flights, jobs[i][3].shape[1]
        return pltpu.make_async_copy(
            buf.at[slot, :, pl.ds(0, width)], jobs[i][3].at[pl.ds(jobs[i][4], tile)], sems.at[slot]
        )

    for i, (left, at, right, out, unused_start) in enumerate(jobs):
        if i >= flights:
            copy(i - flights).wait()
        buf[i % flights, :, : out.shape[1]] = lax.dot_general(
            left[:, at : at + tile], right[...], (((0,), (0,)), ((), ())), preferred_element_type=F32
        )
        copy(i).start()
    for i in range(max(0, len(jobs) - flights), len(jobs)):
        copy(i).wait()


def weight_grads(tile, begin, operands, shapes, ahead, before=()):
    flights, widest = 4, max(shape[1] for shape in shapes)
    slots, hidden = operands[-1].shape[0], 2 * operands[-1].shape[1]
    written = sum(shape[0] * shape[1] for shape in shapes)
    return pl.pallas_call(
        functools.partial(weight_grads_kernel, ahead, begin),
        out_shape=[held(shape, F32) for shape in shapes],
        in_specs=[IN_VMEM] * len(operands) + [IN_PLACE] * len(before),
        out_specs=[IN_PLACE] * len(shapes),
        scratch_shapes=[
            pltpu.VMEM((flights, tile, widest), F32),
            pltpu.SemaphoreType.DMA((flights,)),
            pltpu.VMEM((slots, hidden), BF16),
        ],
        input_output_aliases={len(operands): 0} if before else {},
        compiler_params=params(26),
        cost_estimate=cost(2 * slots * written, 3 * written),
        name="weight_grads",
    )(*operands, *before)


def final_kernel(count, *refs):
    pieces, mine, place, mixed, token_grad = refs[:count], *refs[count:]
    local, width = mixed.shape
    sums = pieces[0][...].astype(F32)
    for piece in pieces[1:]:
        sums = sums + piece[...].astype(F32)
    gates = mine[:local, width : width + 1].astype(F32)
    mixed[...] = (mine[:local, :width].astype(F32) + gates * sums[:local]).astype(BF16)
    slot_grad = (mine[local:, :width].astype(F32) + sums[local:]).astype(BF16)
    token_grad[...] = lax.dot_general(
        place[...], slot_grad, (((0,), (0,)), ((), ())), preferred_element_type=F32
    ).astype(BF16)


def final(pieces, mine, place):
    _, width = pieces[0].shape
    local, tokens = place.shape
    return pl.pallas_call(
        functools.partial(final_kernel, len(pieces)),
        out_shape=[held((local, width), BF16), held((tokens, width), BF16)],
        in_specs=[IN_VMEM] * (len(pieces) + 2),
        out_specs=[IN_VMEM] * 2,
        compiler_params=params(6),
        name="final",
    )(*pieces, mine, place)


def over_chips(total, bit=2):
    while bit < lax.axis_size("tensor"):
        total = total + swap(total.astype(BF16), "tensor", bit).astype(F32)
        bit *= 2
    return total


def per_device(merged, positions, picked, router_score, up_weight, down_weight, mixed_grad):
    local, width = mixed_grad.shape
    seqs, vits = lax.axis_size("seq"), lax.axis_size("vit")
    hidden = up_weight.shape[1]
    piece, place = route(positions, picked, router_score, merged, mixed_grad)
    pieces, up_sent, down_sent, down_kept = gather_pieces(piece, up_weight, down_weight)
    rows, scaled, mine, pre_sent, pre_kept = first(pieces, up_sent, up_weight)
    grad_got = swap(act_grad_half(scaled, down_sent, BF16)[0], "tensor", 1)
    pre_sum = pre_kept + swap(pre_sent, "tensor", 1).astype(F32)
    rounded, scaled = lax.optimization_barrier((pre_sum.astype(BF16), scaled))
    grad_kept, down_kept = act_grad_half(scaled, down_kept, F32, True)
    pre = over_chips(pre_sum + swap(rounded, "tensor", 2).astype(F32), 4)
    act = jax.nn.silu(pre).astype(BF16)
    act, pre = lax.optimization_barrier((act, pre))
    act_other = swap(act, "tensor", 1)
    (down_other,) = load(down_weight, ("other",), hidden // 2, width)
    y = y_terms(act, act_other, down_kept, down_other)
    act_grad = over_chips(grad_kept + grad_got.astype(F32))
    act_grad, y = lax.optimization_barrier((act_grad, y))
    sig = jax.nn.sigmoid(pre)
    pre_grad = (act_grad * sig * (1.0 + pre * (1.0 - sig))).astype(BF16)
    pre_grad_other = swap(pre_grad, "tensor", 1)
    row_own = row_part(pre_grad, up_weight)
    terms = all_terms(pre_grad_other, row_own, y, up_weight, local)

    tile = min(256, hidden // 2, width)
    blocks = width // tile
    early = blocks // 4
    grads = (rows, pre_grad, pre_grad_other)
    down_grad, up_grad = weight_grads(
        tile, (0, early), (act, act_other, scaled, *grads), ((hidden, width), (width, hidden)), True
    )
    terms = sum_over_vit(terms.reshape(vits, seqs, 2 * local, width))
    terms, up_grad = lax.optimization_barrier((terms, up_grad))
    arrived = pieces_over_seq(terms)
    (up_grad,) = weight_grads(tile, (early, blocks), grads, ((width, hidden),), False, (up_grad,))
    mixed, token_grad = final(arrived, mine, place)
    return (mixed, token_grad, up_grad, down_grad)


def solution(mesh):
    return jax.shard_map(
        per_device,
        mesh=mesh,
        in_specs=(
            P(("vit", "seq"), "tensor"),
            P(("vit", "seq")),
            P(("vit", "seq")),
            P(("vit", "seq")),
            P("tensor", ("vit", "seq")),
            P(("vit", "seq"), "tensor"),
            P(("vit", "seq"), "tensor"),
        ),
        out_specs=(
            P(("vit", "seq"), "tensor"),
            P(("vit", "seq"), "tensor"),
            P("tensor", ("vit", "seq")),
            P(("vit", "seq"), "tensor"),
        ),
        check_vma=False,
    )
```

```python
import functools

import jax
import jax.numpy as jnp
from jax import lax
from jax.experimental import pallas as pl
from jax.experimental.pallas import tpu as pltpu
from jax.sharding import PartitionSpec as P


CAP = 2
SPAN = 16384
LANES = 128
MIB = 1 << 20
PARTS = 4

F32 = jnp.float32
BF16 = jnp.bfloat16
VMEM = pltpu.MemorySpace.VMEM
IN_VMEM = pl.BlockSpec(memory_space=VMEM)
IN_HBM = pl.BlockSpec(memory_space=pltpu.MemorySpace.HBM)
IN_PLACE = pl.BlockSpec(memory_space=pl.ANY)
AS_IS = (((1,), (0,)), ((), ()))
TURNED = (((1,), (1,)), ((), ()))


def in_hbm(array):
    return pltpu.with_memory_space_constraint(array, pltpu.MemorySpace.HBM)


def params(mib):
    return pltpu.CompilerParams(vmem_limit_bytes=mib * MIB)


def held(shape, dtype):
    return jax.ShapeDtypeStruct(shape, dtype)


def cost(flops, moved):
    return pl.CostEstimate(flops=int(flops), bytes_accessed=int(moved), transcendentals=0)


def swap(value, axis, bit):
    size = lax.axis_size(axis)
    return lax.ppermute(value, axis, [(i, i ^ bit) for i in range(size)])


def other_half(size):
    return pl.multiple_of((1 - lax.rem(lax.axis_index("tensor"), 2)) * size, size)


def own_half(size):
    return pl.multiple_of(lax.rem(lax.axis_index("tensor"), 2) * size, size)


def load_kernel(wheres, *refs):
    source, outs, sems = refs[0], refs[1:-1], refs[-1]
    copies = []
    for where, out in zip(wheres, outs):
        rows, columns = out.shape
        at = own_half if where == "own" else other_half
        row = at(rows) if rows < source.shape[0] else 0
        column = at(columns) if columns < source.shape[1] else 0
        each = rows // PARTS
        for i in range(PARTS):
            part = source.at[pl.ds(row + i * each, each), pl.ds(column, columns)]
            copies.append(
                pltpu.make_async_copy(part, out.at[pl.ds(i * each, each)], sems.at[len(copies)])
            )
    for copy in copies:
        copy.start()
    for copy in copies:
        copy.wait()


def load(weights, wheres, rows, columns):
    return pl.pallas_call(
        functools.partial(load_kernel, wheres),
        out_shape=[pltpu.VMEM((rows, columns), weights.dtype)] * len(wheres),
        in_specs=[IN_PLACE],
        out_specs=[IN_VMEM] * len(wheres),
        scratch_shapes=[pltpu.SemaphoreType.DMA((PARTS * len(wheres),))],
        compiler_params=params(2),
        cost_estimate=cost(0, 2 * len(wheres) * rows * columns),
        name="load",
    )(in_hbm(weights))


def tick_kernel(value, same):
    same[...] = value[...]


def tick(value):
    return pl.pallas_call(
        tick_kernel,
        out_shape=held(value.shape, value.dtype),
        in_specs=[IN_VMEM],
        out_specs=IN_VMEM,
        compiler_params=params(1),
        name="tick",
    )(value)


def gather_pieces(piece, up, down, place):
    seqs, vits = lax.axis_size("seq"), lax.axis_size("vit")
    deep, hidden = up.shape
    piece, up = lax.optimization_barrier((piece, up))
    along = [piece] + [swap(piece, "seq", k) for k in range(1, seqs)]
    (up,) = load(up, ("other",), deep, hidden // 2)
    near, up, place = lax.optimization_barrier((along[1 : seqs // 2], up, place))
    place = tick(place)
    far, up, down, place = lax.optimization_barrier((along[seqs // 2 :], up, down, place))
    along = [piece] + near + far
    out = list(along)
    for v in range(1, vits):
        out += [swap(p, "vit", v) for p in along]
    sent, kept = load(down, ("other", "own"), hidden // 2, deep)
    return (out, place, *lax.optimization_barrier((up, sent, kept)))


def sum_over_vit(blocks):
    v = lax.axis_index("vit")
    total = lax.dynamic_index_in_dim(blocks, v, 0, False).astype(F32)
    for k in range(1, lax.axis_size("vit")):
        total = total + swap(lax.dynamic_index_in_dim(blocks, v ^ k, 0, False), "vit", k).astype(F32)
    return total.astype(BF16)


def pieces_over_seq(blocks):
    s = lax.axis_index("seq")
    out = [lax.dynamic_index_in_dim(blocks, s, 0, False)]
    for k in range(1, lax.axis_size("seq")):
        out.append(swap(lax.dynamic_index_in_dim(blocks, s ^ k, 0, False), "seq", k))
    return out


def route_kernel(seqs, *refs):
    sources, (piece, place), copied, sems = refs[:5], refs[5:7], refs[7:12], refs[12]
    copies = [pltpu.make_async_copy(sources[i], copied[i], sems.at[i]) for i in range(5)]
    for copy in copies:
        copy.start()
    for copy in copies[:3]:
        copy.wait()
    pos, picked, score, merged, cotangent = copied
    local, tokens = place.shape
    width = merged.shape[1]
    taken = picked[...] == 1
    target = lax.shift_right_logical(pos[...], SPAN.bit_length() - 1)
    owner = lax.broadcasted_iota(jnp.int32, (seqs, tokens), 0)
    onehot = jnp.where((owner == target) & taken, 1.0, 0.0)
    before = lax.broadcasted_iota(jnp.int32, (tokens, tokens), 0) < lax.broadcasted_iota(
        jnp.int32, (tokens, tokens), 1
    )
    before = jnp.where(before, 1.0, 0.0).astype(BF16)
    earlier = jnp.dot(onehot.astype(BF16), before, preferred_element_type=F32)
    rank = jnp.sum(earlier * onehot, axis=0, keepdims=True)
    slot = target.astype(F32) * CAP + rank
    wanted = lax.broadcasted_iota(jnp.int32, (local, tokens), 0).astype(F32)
    chosen = jnp.where((wanted == slot) & taken, 1.0, 0.0)
    place[...] = chosen.astype(BF16)
    gate = jax.nn.sigmoid(score[...]).astype(BF16).astype(F32)
    gates = jnp.sum(chosen * gate, axis=1, keepdims=True)
    piece[0:local, width : width + LANES] = jnp.broadcast_to(gates, (local, LANES)).astype(BF16)
    for copy in copies[3:]:
        copy.wait()
    rows = jnp.dot(chosen.astype(BF16), merged[...], preferred_element_type=F32)
    piece[0:local, 0:width] = rows.astype(BF16)
    piece[local : 2 * local, 0:width] = cotangent[...]
    piece[local : 2 * local, width : width + LANES] = jnp.zeros((local, LANES), BF16)


def route(positions, picked, score, merged, cotangent):
    local, width = cotangent.shape
    tokens = merged.shape[0]
    arrays = (positions[None], picked[None], score[None], merged, cotangent)
    return pl.pallas_call(
        functools.partial(route_kernel, lax.axis_size("seq")),
        out_shape=[pltpu.VMEM((2 * local, width + LANES), BF16), held((local, tokens), BF16)],
        in_specs=[IN_HBM] * 5,
        out_specs=[IN_VMEM] * 2,
        scratch_shapes=[pltpu.VMEM(a.shape, a.dtype) for a in arrays] + [pltpu.SemaphoreType.DMA((5,))],
        compiler_params=params(4),
        name="route",
    )(*[in_hbm(a) for a in arrays])


def product(left, weights, turned, start, size, out):
    tile = min(512, size)

    def step(j, carry):
        src = pl.ds(pl.multiple_of(start + j * tile, tile), tile)
        part = weights[src, :] if turned else weights[:, src]
        term = lax.dot_general(left, part, TURNED if turned else AS_IS, preferred_element_type=F32)
        out[:, pl.ds(pl.multiple_of(j * tile, tile), tile)] = term.astype(out.dtype)
        return carry

    lax.fori_loop(0, size // tile, step, 0)


def first_kernel(seqs, count, *refs):
    pieces, up_sent, up = refs[:count], refs[count], refs[count + 1]
    rows, scaled, mine, sent, kept, together, chunks, sems = refs[count + 2 :]
    slots, width = rows.shape
    half = sent.shape[1]
    coming = Stream(up, False, 0, own_half(half), chunks, sems)
    local = slots // count
    v, s = lax.axis_index("vit"), lax.axis_index("seq")
    me = v * seqs + s
    for k in range(count):
        together[2 * local * k : 2 * local * (k + 1), :] = pieces[k][...]
    total = 2 * slots
    c = lax.broadcasted_iota(jnp.int32, (1, total), 1)
    dev = (c // (2 * local)) ^ me
    j = c % (2 * local)
    slot_row = ((dev // seqs) * seqs + j // CAP) * local + (dev % seqs) * CAP + j % CAP
    slot = jnp.where(j < local, slot_row, slots + dev * local + j - local)
    wanted = lax.broadcasted_iota(jnp.int32, (total, total), 0)
    order = jnp.where(wanted == slot, 1.0, 0.0).astype(BF16)
    data = together[...]
    got = jnp.dot(order, data, preferred_element_type=F32)
    i = lax.broadcasted_iota(jnp.int32, (2 * local, total), 0)
    own = slots + (v * seqs + (i - local) // CAP) * local + s * CAP + i % CAP
    own = jnp.where(i < local, me * local + i, own)
    pick = jnp.where(own == slot, 1.0, 0.0).astype(BF16)
    mine[...] = jnp.dot(pick, data, preferred_element_type=F32).astype(BF16)
    rows[...] = got[:slots, :width].astype(BF16)
    scaled[...] = (got[:slots, width : width + 1] * got[slots:, :width]).astype(BF16)
    product(rows[...], up_sent, False, 0, half, sent)

    def store(where, value):
        kept[:, where] = value

    coming.finish(rows, store)


def first(pieces, up_sent, up):
    count = len(pieces)
    two, wide = pieces[0].shape
    slots, width = count * two // 2, wide - LANES
    half = up.shape[1] // 2
    return pl.pallas_call(
        functools.partial(first_kernel, lax.axis_size("seq"), count),
        out_shape=[
            held((slots, width), BF16),
            held((slots, width), BF16),
            held((two, wide), BF16),
            held((slots, half), BF16),
            held((slots, half), F32),
        ],
        in_specs=[IN_VMEM] * (count + 1) + [IN_PLACE],
        out_specs=[IN_VMEM] * 5,
        scratch_shapes=[pltpu.VMEM((2 * slots, wide), BF16), *stream_scratch(up, False, width, half)],
        compiler_params=params(6 + (30 * slots * wide + 2 * width * half) // MIB),
        cost_estimate=cost(2 * slots * up.size, 2 * up.size),
        name="first",
    )(*pieces, up_sent, in_hbm(up))


def act_grad_kernel(scaled, down, out, *again):
    if again:
        copy = pltpu.make_async_copy(down, again[0], again[1])
        copy.start()
    product(scaled[...], down, True, 0, out.shape[1], out)
    if again:
        copy.wait()


def act_grad_half(scaled, down, dtype, again=False):
    slots, half = scaled.shape[0], down.shape[0]
    return pl.pallas_call(
        act_grad_kernel,
        out_shape=[held((slots, half), dtype)] + [pltpu.VMEM(down.shape, down.dtype)] * again,
        in_specs=[IN_VMEM] * 2,
        out_specs=[IN_VMEM] * (1 + again),
        scratch_shapes=[pltpu.SemaphoreType.DMA] * again,
        compiler_params=params(6 + 12 * slots * half // MIB),
        cost_estimate=cost(2 * slots * down.size, 2 * down.size),
        name="act_grad",
    )(scaled, down)


class Stream:
    def __init__(self, weights, turned, row, column, chunks, sems):
        self.turned, self.chunks, self.sems = turned, chunks, sems
        count, tall, wide = chunks.shape
        self.copies = []
        for i in range(count):
            begin = (row + i * tall, column) if turned else (row, column + i * wide)
            source = weights.at[pl.ds(begin[0], tall), pl.ds(begin[1], wide)]
            self.copies.append(pltpu.make_async_copy(source, chunks.at[i], sems.at[i]))
        for copy in self.copies:
            copy.start()

    def finish(self, left, store):
        value = left[...]
        _, tall, wide = self.chunks.shape
        tile = tall if self.turned else wide
        for i, copy in enumerate(self.copies):
            copy.wait()
            store(
                slice(i * tile, (i + 1) * tile),
                lax.dot_general(
                    value,
                    self.chunks[i],
                    TURNED if self.turned else AS_IS,
                    preferred_element_type=F32,
                ),
            )


def stream_scratch(weights, turned, deep, across):
    tile = min(512, across)
    count = across // tile
    shape = (count, tile, deep) if turned else (count, deep, tile)
    return [pltpu.VMEM(shape, weights.dtype), pltpu.SemaphoreType.DMA((count,))]


def y_kernel(own, other, down_own, down_other, out):
    y = jnp.dot(own[...], down_own[...], preferred_element_type=F32)
    y = y + jnp.dot(other[...], down_other[...], preferred_element_type=F32)
    out[...] = y.astype(out.dtype)


def y_terms(own, other, down_own, down_other):
    slots, half = own.shape
    width = down_own.shape[1]
    return pl.pallas_call(
        y_kernel,
        out_shape=held((slots, width), BF16),
        in_specs=[IN_VMEM] * 4,
        out_specs=IN_VMEM,
        compiler_params=params(6 + 24 * slots * width // MIB),
        cost_estimate=cost(4 * slots * half * width, 4 * half * width),
        name="y",
    )(own, other, down_own, down_other)


def row_kernel(own, up, out, chunks, sems):
    coming = Stream(up, True, 0, own_half(own.shape[1]), chunks, sems)

    def store(where, value):
        out[:, where] = value

    coming.finish(own, store)


def row_part(own, up):
    slots, half = own.shape
    width = up.shape[0]
    return pl.pallas_call(
        row_kernel,
        out_shape=held((slots, width), F32),
        in_specs=[IN_VMEM, IN_PLACE],
        out_specs=IN_VMEM,
        scratch_shapes=stream_scratch(up, True, half, width),
        compiler_params=params(6 + (up.size + 24 * slots * width) // MIB),
        cost_estimate=cost(slots * up.size, up.size),
        name="row_part",
    )(own, in_hbm(up))


def terms_kernel(seqs, local, other, before, y, up, terms, chunks, sems, term):
    slots, half = other.shape
    coming = Stream(up, True, 0, other_half(half), chunks, sems)
    r = lax.broadcasted_iota(jnp.int32, (2 * slots, 1), 0)
    d, j = r // (2 * local), r % (2 * local)
    src = ((d // seqs) * seqs + (j - local) // CAP) * local + (d % seqs) * CAP + j % CAP
    src = jnp.where(j < local, d * local + j, slots + src)
    order = jnp.where(src == lax.broadcasted_iota(jnp.int32, (2 * slots, 2 * slots), 1), 1.0, 0.0)
    order = order.astype(BF16)
    term[:slots, :] = y[...]

    def store(where, value):
        term[slots:, where] = (value + before[:, where]).astype(BF16)
        both = jnp.dot(order, term[:, where], preferred_element_type=F32)
        terms[:, where] = both.astype(BF16)

    coming.finish(other, store)


def all_terms(other, before, y, up, local):
    slots, half = other.shape
    width = up.shape[0]
    return pl.pallas_call(
        functools.partial(terms_kernel, lax.axis_size("seq"), local),
        out_shape=held((2 * slots, width), BF16),
        in_specs=[IN_VMEM] * 3 + [IN_PLACE],
        out_specs=IN_VMEM,
        scratch_shapes=[
            *stream_scratch(up, True, half, width),
            pltpu.VMEM((2 * slots, width), BF16),
        ],
        compiler_params=params(6 + (up.size + 32 * slots * width) // MIB),
        cost_estimate=cost(slots * up.size, up.size),
        name="all_terms",
    )(other, before, y, in_hbm(up))


def weight_grads_kernel(ahead, begin, *refs):
    if ahead:
        act, act_other, scaled, rows, own, other, down_grad, up_grad, buf, sems, whole = refs
    else:
        rows, own, other, _, up_grad, buf, sems, whole = refs
    half = own.shape[1]
    flights, tile = buf.shape[0], buf.shape[1]
    whole[:, pl.ds(own_half(half), half)] = own[...]
    whole[:, pl.ds(other_half(half), half)] = other[...]
    jobs = []
    if ahead:
        each = half // tile
        for i in range(2 * each):
            left, start = (act, own_half(half)) if i < each else (act_other, other_half(half))
            jobs.append((left, (i % each) * tile, scaled, down_grad, start + (i % each) * tile))
    for i in range(*begin):
        jobs.append((rows, i * tile, whole, up_grad, i * tile))

    def copy(i):
        slot, width = i % flights, jobs[i][3].shape[1]
        return pltpu.make_async_copy(
            buf.at[slot, :, pl.ds(0, width)], jobs[i][3].at[pl.ds(jobs[i][4], tile)], sems.at[slot]
        )

    for i, (left, at, right, out, unused_start) in enumerate(jobs):
        if i >= flights:
            copy(i - flights).wait()
        buf[i % flights, :, : out.shape[1]] = lax.dot_general(
            left[:, at : at + tile], right[...], (((0,), (0,)), ((), ())), preferred_element_type=F32
        )
        copy(i).start()
    for i in range(max(0, len(jobs) - flights), len(jobs)):
        copy(i).wait()


def weight_grads(tile, begin, operands, shapes, ahead, before=()):
    flights, widest = 4, max(shape[1] for shape in shapes)
    slots, hidden = operands[-1].shape[0], 2 * operands[-1].shape[1]
    written = sum(shape[0] * shape[1] for shape in shapes)
    return pl.pallas_call(
        functools.partial(weight_grads_kernel, ahead, begin),
        out_shape=[held(shape, F32) for shape in shapes],
        in_specs=[IN_VMEM] * len(operands) + [IN_PLACE] * len(before),
        out_specs=[IN_PLACE] * len(shapes),
        scratch_shapes=[
            pltpu.VMEM((flights, tile, widest), F32),
            pltpu.SemaphoreType.DMA((flights,)),
            pltpu.VMEM((slots, hidden), BF16),
        ],
        input_output_aliases={len(operands): 0} if before else {},
        compiler_params=params(26),
        cost_estimate=cost(2 * slots * written, 3 * written),
        name="weight_grads",
    )(*operands, *before)


def final_kernel(count, *refs):
    pieces, mine, place, mixed, token_grad = refs[:count], *refs[count:]
    local, width = mixed.shape
    sums = pieces[0][...].astype(F32)
    for piece in pieces[1:]:
        sums = sums + piece[...].astype(F32)
    gates = mine[:local, width : width + 1].astype(F32)
    mixed[...] = (mine[:local, :width].astype(F32) + gates * sums[:local]).astype(BF16)
    slot_grad = (mine[local:, :width].astype(F32) + sums[local:]).astype(BF16)
    token_grad[...] = lax.dot_general(
        place[...], slot_grad, (((0,), (0,)), ((), ())), preferred_element_type=F32
    ).astype(BF16)


def final(pieces, mine, place):
    _, width = pieces[0].shape
    local, tokens = place.shape
    return pl.pallas_call(
        functools.partial(final_kernel, len(pieces)),
        out_shape=[held((local, width), BF16), held((tokens, width), BF16)],
        in_specs=[IN_VMEM] * (len(pieces) + 2),
        out_specs=[IN_VMEM] * 2,
        compiler_params=params(6),
        name="final",
    )(*pieces, mine, place)


def over_chips(total, bit=2):
    while bit < lax.axis_size("tensor"):
        total = total + swap(total.astype(BF16), "tensor", bit).astype(F32)
        bit *= 2
    return total


def per_device(merged, positions, picked, router_score, up_weight, down_weight, mixed_grad):
    local, width = mixed_grad.shape
    seqs, vits = lax.axis_size("seq"), lax.axis_size("vit")
    hidden = up_weight.shape[1]
    piece, place = route(positions, picked, router_score, merged, mixed_grad)
    pieces, place, up_sent, down_sent, down_kept = gather_pieces(piece, up_weight, down_weight, place)
    rows, scaled, mine, pre_sent, pre_kept = first(pieces, up_sent, up_weight)
    grad_got = swap(act_grad_half(scaled, down_sent, BF16)[0], "tensor", 1)
    pre_sum = pre_kept + swap(pre_sent, "tensor", 1).astype(F32)
    rounded, scaled = lax.optimization_barrier((pre_sum.astype(BF16), scaled))
    grad_kept, down_kept = act_grad_half(scaled, down_kept, F32, True)
    pre = over_chips(pre_sum + swap(rounded, "tensor", 2).astype(F32), 4)
    act = jax.nn.silu(pre).astype(BF16)
    act, pre = lax.optimization_barrier((act, pre))
    act_other = swap(act, "tensor", 1)
    (down_other,) = load(down_weight, ("other",), hidden // 2, width)
    y = y_terms(act, act_other, down_kept, down_other)
    act_grad = over_chips(grad_kept + grad_got.astype(F32))
    act_grad, y = lax.optimization_barrier((act_grad, y))
    sig = jax.nn.sigmoid(pre)
    pre_grad = (act_grad * sig * (1.0 + pre * (1.0 - sig))).astype(BF16)
    pre_grad_other = swap(pre_grad, "tensor", 1)
    row_own = row_part(pre_grad, up_weight)
    terms = all_terms(pre_grad_other, row_own, y, up_weight, local)

    tile = min(256, hidden // 2, width)
    blocks = width // tile
    early = blocks // 4
    grads = (rows, pre_grad, pre_grad_other)
    down_grad, up_grad = weight_grads(
        tile, (0, early), (act, act_other, scaled, *grads), ((hidden, width), (width, hidden)), True
    )
    terms = sum_over_vit(terms.reshape(vits, seqs, 2 * local, width))
    terms, up_grad = lax.optimization_barrier((terms, up_grad))
    arrived = pieces_over_seq(terms)
    (up_grad,) = weight_grads(tile, (early, blocks), grads, ((width, hidden),), False, (up_grad,))
    mixed, token_grad = final(arrived, mine, place)
    return (mixed, token_grad, up_grad, down_grad)


def solution(mesh):
    return jax.shard_map(
        per_device,
        mesh=mesh,
        in_specs=(
            P(("vit", "seq"), "tensor"),
            P(("vit", "seq")),
            P(("vit", "seq")),
            P(("vit", "seq")),
            P("tensor", ("vit", "seq")),
            P(("vit", "seq"), "tensor"),
            P(("vit", "seq"), "tensor"),
        ),
        out_specs=(
            P(("vit", "seq"), "tensor"),
            P(("vit", "seq"), "tensor"),
            P("tensor", ("vit", "seq")),
            P(("vit", "seq"), "tensor"),
        ),
        check_vma=False,
    )
```
